32 devices in a mesh: grp: 2 (over y), seq: 8 (over z, x), doc: 2 (over core).
Axes of the slice: x: 2, y: 2, z: 4, core: 2. Of those that a mesh axis runs over, the one named last changes fastest.
Arguments:
- state: bfloat16 [32, 3, 1024, 1024], P(('grp', 'seq', 'doc')), parts along dimension 0, may hold values from -0.1875 to 0.1875
- keys: bfloat16 [2, 32, 384, 1024], P(None, ('grp', 'seq', 'doc')), parts along dimension 1, may hold values from -6 to 6
- values: bfloat16 [2, 32, 384, 1024], P(None, ('grp', 'seq', 'doc')), parts along dimension 1, may hold values from -6 to 6
- queries: bfloat16 [2, 32, 384, 1024], P(None, ('grp', 'seq', 'doc')), parts along dimension 1, may hold values from -6 to 6
- rates: float32 [2, 32, 384], P(None, 'grp'), parts along dimension 1, may hold values from 0.001 to 0.01
- remaining: int32 [32], P('grp'), parts along dimension 0, may hold values from 1 to 2
- first_owner: int32 [32], P('grp'), parts along dimension 0, may hold values from 0 to 15, each once
- migration: int32 [32], P('grp'), parts along dimension 0, may hold values from 0 to 15, as said below
Outputs:
- round_one: bfloat16 [32, 384, 1024], P(('grp', 'seq', 'doc')), parts along dimension 0
- round_two: bfloat16 [32, 384, 1024], P(('grp', 'seq', 'doc')), parts along dimension 0
The draws below stay inside these ranges and needn't reach their ends.
There are 2 independent parts, one for each index of `grp`. The reference program is written for one: setup_inputs(seed, part) draws one part's arguments, and reference() takes and returns one part's arrays. A program takes and returns all parts, laid end to end along the dimension named above; each array names one. Nothing has to cross between parts.
Inputs may be any that keep to these rules, and one draw needn't show every extreme that they name: first_owner is a permutation: document d starts with the fast weights state[first_owner[d]]. migration is a permutation that leaves all but exactly 4 owners in place. `remaining`: a document has a round-two block exactly where its entry is 2.
All inputs are finite; a program needn't handle non-finite values.
Results may differ from the reference program's by a relative error of at most 0.012.
Values may be sent and summed in bfloat16 or wider, within the bound.
A program may use at most 128 MiB of HBM per device.

```python
import math
import jax
import jax.numpy as jnp
from jax import lax

D = 1024
CH = 384
ROUNDS = 2
DOCS = 16
OWNERS = 16


def draw_migration(key, part):
    shuffled = jax.random.permutation(key, OWNERS).astype(jnp.int32)
    moving = OWNERS // 4
    chosen = shuffled[:moving]
    target = jnp.roll(chosen, 1)
    initial = jnp.arange(OWNERS, dtype=jnp.int32)
    return initial.at[chosen].set(target).astype(jnp.int32)


def plant(entries, rng, low, top_value):
    dims = entries.shape
    index_at = [jax.random.randint(jax.random.fold_in(rng, axis), (), 0, dims[axis]) for axis in range(len(dims))]
    entries = entries.at[tuple(index_at)].set(low)
    longest = dims.index(max(dims))
    index_at[longest] = (index_at[longest] + 1) % dims[longest]
    return entries.at[tuple(index_at)].set(top_value)


def steps_of(own_key, extent, split, low, top_value):
    level, own = 1.0, jax.random.fold_in(own_key, 6)
    for dim, blocks in split:
        steps = jnp.exp(jax.random.uniform(jax.random.fold_in(own, dim), (blocks,), jnp.float32, low / len(split), top_value / len(split)))
        level = level * jnp.repeat(steps, extent[dim] // blocks).reshape([-1 if axis == dim else 1 for axis in range(len(extent))])
    return level


def centred(stream_key, shape, width, bound, split=(), kind=jnp.bfloat16):
    result = width * jax.random.normal(stream_key, shape, jnp.float32)
    if split:
        result = result * steps_of(stream_key, shape, split, -0.22, 0.18)
    return jnp.clip(result, -bound, bound).astype(kind)


def setup_inputs(seed: int = 0, part: int = 0) -> dict:
    arg_keys = jax.random.split(jax.random.key(seed), 9)
    own_keys = jax.random.split(jax.random.fold_in(arg_keys[8], part), 9)
    state = centred(own_keys[0], (OWNERS, 3, D, D), D ** -0.5, 0.1875, ((0, 16),))
    keys = centred(own_keys[1], (ROUNDS, DOCS, CH, D), 1.0, 6.0, ((1, 16),))
    values = centred(own_keys[2], (ROUNDS, DOCS, CH, D), 1.0, 6.0, ((1, 16),))
    queries = centred(own_keys[3], (ROUNDS, DOCS, CH, D), 1.0, 6.0, ((1, 16),))
    rates = jnp.clip(jnp.exp(jax.random.uniform(own_keys[4], (ROUNDS, DOCS, CH), jnp.float32, math.log(0.001), math.log(0.01))), 0.001, 0.01)
    remaining = plant(jax.random.randint(own_keys[5], (DOCS,), 1, 3), jax.random.fold_in(own_keys[5], 1), 1, 2).astype(jnp.int32)
    first_owner = jax.random.permutation(own_keys[6], DOCS).astype(jnp.int32)
    migration = draw_migration(jax.random.fold_in(jax.random.fold_in(arg_keys[8], part), 71), part)
    return {"state": state, "keys": keys, "values": values, "queries": queries, "rates": rates, "remaining": remaining, "first_owner": first_owner, "migration": migration}


EPSILON = 1e-06

def swiglu_apply(weights, inputs):
    gate_pre = jnp.dot(inputs, weights[0], preferred_element_type=jnp.float32)
    upward = jnp.dot(inputs, weights[1], preferred_element_type=jnp.float32)
    hidden = (jax.nn.silu(gate_pre) * upward).astype(jnp.bfloat16)
    return jnp.dot(hidden, weights[2], preferred_element_type=jnp.float32)

def renorm(weight, gradient):
    before = weight.astype(jnp.float32)
    stepped = before - gradient
    factor = jnp.sqrt(lax.optimization_barrier(jnp.mean(before * before, axis=0)) + EPSILON) / jnp.sqrt(lax.optimization_barrier(jnp.mean(stepped * stepped, axis=0)) + EPSILON)
    return (stepped * factor[None, :]).astype(jnp.bfloat16)

def fast_update(weights, keys_rows, values_rows, rate_rows):
    gate_pre = jnp.dot(keys_rows, weights[0], preferred_element_type=jnp.float32)
    upward = jnp.dot(keys_rows, weights[1], preferred_element_type=jnp.float32)
    sigmoid_gate = jax.nn.sigmoid(gate_pre)
    active = gate_pre * sigmoid_gate
    hidden = (active * upward).astype(jnp.bfloat16)
    scaled_values = (rate_rows[:, None] * values_rows.astype(jnp.float32)).astype(jnp.bfloat16)
    grad_down = -jnp.dot(hidden.T, scaled_values, preferred_element_type=jnp.float32)
    grad_hidden = -jnp.dot(scaled_values, weights[2].T, preferred_element_type=jnp.float32)
    slope = sigmoid_gate * (1.0 + gate_pre * (1.0 - sigmoid_gate))
    grad_gate = (grad_hidden * upward * slope).astype(jnp.bfloat16)
    grad_up = (grad_hidden * active).astype(jnp.bfloat16)
    grad_first = jnp.dot(keys_rows.T, grad_gate, preferred_element_type=jnp.float32)
    grad_third = jnp.dot(keys_rows.T, grad_up, preferred_element_type=jnp.float32)
    return jnp.stack([renorm(weights[0], grad_first), renorm(weights[1], grad_third), renorm(weights[2], grad_down)])

def inverse_of(permuted):
    count = permuted.shape[0]
    labels = jnp.arange(count, dtype=jnp.int32)
    return lax.optimization_barrier(jnp.sum(jnp.where(permuted[None, :] == labels[:, None], labels[None, :], 0), axis=1)).astype(jnp.int32)

def reference(state, keys, values, queries, rates, remaining, first_owner, migration):
    doc_ids = jnp.arange(DOCS, dtype=jnp.int32)

    def one_doc(doc_index):
        owner_now = first_owner[doc_index]
        first_state = fast_update(state[owner_now], keys[0, doc_index], values[0, doc_index], rates[0, doc_index])
        out_first = swiglu_apply(first_state, queries[0, doc_index]).astype(jnp.bfloat16)
        second_state = fast_update(first_state, keys[1, doc_index], values[1, doc_index], rates[1, doc_index])
        out_second = swiglu_apply(second_state, queries[1, doc_index])
        is_live = remaining[doc_index] >= 2
        out_second = jnp.where(is_live, out_second, jnp.float32(0.0)).astype(jnp.bfloat16)
        return (out_first, out_second)
    round_one, by_doc = lax.map(one_doc, doc_ids)
    doc_second = inverse_of(migration[first_owner])
    round_two = jnp.take(by_doc, doc_second, axis=0)
    return (round_one, round_two)
```

```python
import jax
import jax.numpy as jnp
from jax import lax
from jax.experimental import pallas as pl
from jax.experimental.pallas import tpu as pltpu
from jax.sharding import PartitionSpec as P

EPSILON = 1e-06
AXES = ("seq", "doc")
HALVES = 2
AHEAD = 2


def shortened(array):

    def short(part):
        return part.astype(jnp.bfloat16) if part.dtype == jnp.float32 else part

    return jax.tree.map(short, array)


def swiglu_apply(weights, inputs):
    gate_pre = jnp.dot(inputs, weights[0], preferred_element_type=jnp.float32)
    upward = jnp.dot(inputs, weights[1], preferred_element_type=jnp.float32)
    hidden = (jax.nn.silu(gate_pre) * upward).astype(jnp.bfloat16)
    return jnp.dot(hidden, weights[2], preferred_element_type=jnp.float32)


def renorm(weight, gradient):
    before = weight.astype(jnp.float32)
    stepped = before - gradient
    factor = jnp.sqrt(jnp.mean(before * before, axis=0) + EPSILON) / jnp.sqrt(
        jnp.mean(stepped * stepped, axis=0) + EPSILON
    )
    return (stepped * factor[None, :]).astype(jnp.bfloat16)


def fast_update(weights, keys_rows, values_rows, rate_rows):
    gate_pre = jnp.dot(keys_rows, weights[0], preferred_element_type=jnp.float32)
    upward = jnp.dot(keys_rows, weights[1], preferred_element_type=jnp.float32)
    sigmoid_gate = jax.nn.sigmoid(gate_pre)
    active = gate_pre * sigmoid_gate
    hidden = (active * upward).astype(jnp.bfloat16)
    scaled_values = (rate_rows[:, None] * values_rows.astype(jnp.float32)).astype(jnp.bfloat16)
    grad_down = -jnp.dot(hidden.T, scaled_values, preferred_element_type=jnp.float32)
    grad_hidden = -jnp.dot(scaled_values, weights[2].T, preferred_element_type=jnp.float32)
    slope = sigmoid_gate * (1.0 + gate_pre * (1.0 - sigmoid_gate))
    grad_gate = (grad_hidden * upward * slope).astype(jnp.bfloat16)
    grad_up = (grad_hidden * active).astype(jnp.bfloat16)
    grad_first = jnp.dot(keys_rows.T, grad_gate, preferred_element_type=jnp.float32)
    grad_third = jnp.dot(keys_rows.T, grad_up, preferred_element_type=jnp.float32)
    return jnp.stack(
        [
            renorm(weights[0], grad_first),
            renorm(weights[1], grad_third),
            renorm(weights[2], grad_down),
        ]
    )


def inverse_of(permuted):
    count = permuted.shape[0]
    labels = jnp.arange(count, dtype=jnp.int32)
    return jnp.sum(jnp.where(permuted[None, :] == labels[:, None], labels[None, :], 0), axis=1)


def move_rows(items):
    return jax.tree.map(
        lambda part, own: part.astype(own.dtype),
        lax.all_to_all(shortened(items), ("seq", "doc"), split_axis=0, concat_axis=0, tiled=True),
        items,
    )


def send_back(pieces):
    return lax.all_to_all(pieces, ("seq", "doc"), split_axis=0, concat_axis=0, tiled=True)


def move_result(pieces):
    return lax.all_to_all(pieces, ("seq", "doc"), split_axis=0, concat_axis=0, tiled=True)


def route_kernel(slab, chunks, cross, cross_idx, own_idx, outer_idx, *refs):
    tensors = 3
    sources, refs = refs[:tensors], refs[tensors:]
    outs, refs = refs[: chunks // HALVES], refs[chunks // HALVES :]
    held, refs = refs[:chunks], refs[chunks:]
    crossing, refs = refs[:chunks], refs[chunks:]
    crossed, refs = refs[:chunks], refs[chunks:]
    returning, refs = refs[:chunks], refs[chunks:]
    final, refs = refs[:chunks], refs[chunks:]
    local_in, local_out, deal_s, deal_r, in_s, in_r, mid_s, mid_r, back_s, back_r, last_s, last_r = refs
    cores = lax.axis_size("doc")
    me = lax.axis_index("seq") * cores + lax.axis_index("doc")
    here, member = me // slab, me % slab
    inner = (here == 1) | (here == 2)
    outer = (here == 0) | (here == 3)
    beside = here + 1 - 2 * (here % 2)
    opposite = 3 - here

    def device(which, who):
        index = which * slab + who
        return {"seq": index // cores, "doc": index % cores}

    def remote(src, dst, send, recv, target):
        return pltpu.make_async_remote_copy(
            src_ref=src, dst_ref=dst, send_sem=send, recv_sem=recv,
            device_id=target, device_id_type=pl.DeviceIdType.MESH,
        )

    def source(c):
        block, half = c // HALVES, c % HALVES
        return sources[block % tensors].at[block // tensors * HALVES + half]

    def deal(c):
        copies = []
        for r in range(1, slab):
            who = (member + r) % slab
            copies.append(remote(source(c).at[who], held[c].at[member], deal_s.at[c, r - 1], deal_r.at[c, r - 1], device(here, who)))
        return copies, pltpu.make_async_copy(source(c).at[member], held[c].at[member], local_in.at[c])

    def inward(c):
        return remote(held[c].at[pl.ds(0, slab)], held[c].at[pl.ds(slab, slab)], in_s.at[c], in_r.at[c], device(beside, member))

    def middle(c):
        return remote(crossing[c], crossed[c], mid_s.at[c], mid_r.at[c], device(opposite, member))

    def backward(c):
        return remote(returning[c], final[c], back_s.at[c], back_r.at[c], device(beside, member))

    def last(c):
        target = outs[c // HALVES].at[c % HALVES]
        copies = []
        for r in range(1, slab):
            who = (member + r) % slab
            copies.append(remote(final[c].at[who], target.at[member], last_s.at[c, r - 1], last_r.at[c, r - 1], device(here, who)))
        return copies, pltpu.make_async_copy(final[c].at[member], target.at[member], local_out.at[c])

    def start_all(group):
        for copy in group[0]:
            copy.start()
        group[1].start()

    barrier = pltpu.get_barrier_semaphore()
    for r in range(1, slab):
        pl.semaphore_signal(barrier, inc=1, device_id=device(here, (member + r) % slab), device_id_type=pl.DeviceIdType.MESH)
    pl.semaphore_signal(barrier, inc=1, device_id=device(beside, member), device_id_type=pl.DeviceIdType.MESH)

    @pl.when(inner)
    def _():
        pl.semaphore_signal(barrier, inc=1, device_id=device(opposite, member), device_id_type=pl.DeviceIdType.MESH)
        pl.semaphore_wait(barrier, slab + 1)

    @pl.when(outer)
    def _():
        pl.semaphore_wait(barrier, slab)

    for c in range(min(AHEAD, chunks)):
        start_all(deal(c))
    for t in range(chunks + 5):
        if t + AHEAD < chunks:
            start_all(deal(t + AHEAD))
        if t < chunks:
            copies, mine = deal(t)
            for copy in copies:
                copy.wait_recv()
            mine.wait()

        @pl.when(outer)
        def _():
            if t < chunks:
                inward(t).start()
            c = t - 5
            if 0 <= c < chunks:
                backward(c).wait_recv()
                start_all(last(c))

        @pl.when(inner)
        def _():
            c = t - 1
            if 0 <= c < chunks:
                inward(c).wait_recv()
                for j in range(cross):
                    crossing[c][j] = held[c][cross_idx[j]]
                middle(c).start()
            c = t - 3
            if 0 <= c < chunks:
                middle(c).wait_recv()

                def pick(index):
                    near = held[c][jnp.minimum(index, 2 * slab - 1)]
                    far = crossed[c][jnp.maximum(index - 2 * slab, 0)]
                    return jnp.where(index < 2 * slab, near, far)

                for j in range(slab):
                    returning[c][j] = pick(outer_idx[j])
                backward(c).start()
                for j in range(slab):
                    final[c][j] = pick(own_idx[j])
                start_all(last(c))

    for c in range(chunks):
        for copy in deal(c)[0]:
            copy.wait_send()
        copies, mine = last(c)
        for copy in copies:
            copy.wait_send()
            copy.wait_recv()
        mine.wait()

        @pl.when(outer)
        def _():
            inward(c).wait_send()

        @pl.when(inner)
        def _():
            middle(c).wait_send()
            backward(c).wait_send()


def route_inputs(keys, values, queries, first_owner, doc_first):
    devices = lax.axis_size(AXES)
    slab = devices // 4
    rounds, _, block_rows, width = keys.shape
    rows = block_rows // (HALVES * slab)
    chunks = rounds * 3 * HALVES
    me = lax.axis_index(AXES)
    here = jnp.clip(me // slab, 1, 2)
    outer = jnp.where(here == 1, 0, 3)
    ids = jnp.arange(devices, dtype=jnp.int32)
    goes = (ids // (2 * slab)) != (first_owner // (2 * slab))
    low = ids < 2 * slab
    order = jnp.where(low, (ids + slab) % (2 * slab), ids - 2 * slab)
    before = goes[None, :] & (low[None, :] == low[:, None]) & (order[None, :] < order[:, None])
    rank = jnp.sum(before.astype(jnp.int32), axis=1)
    mine = low == (here == 1)
    slot = jnp.where(mine, order, 2 * slab + rank)
    j = jnp.arange(2 * slab, dtype=jnp.int32)
    hit = goes[None, :] & mine[None, :] & (rank[None, :] == j[:, None])
    cross_idx = jnp.sum(jnp.where(hit, order[None, :], 0), axis=1).astype(jnp.int32)
    is_doc = doc_first[:, None] == ids[None, :]
    owner_slot = jnp.sum(jnp.where(is_doc, slot[None, :], 0), axis=1).astype(jnp.int32)
    own_idx = lax.dynamic_slice(owner_slot, (here * slab,), (slab,))
    outer_idx = lax.dynamic_slice(owner_slot, (outer * slab,), (slab,))
    count = jnp.sum((goes & low).astype(jnp.int32))
    groups = lax.axis_size("grp")
    most = count
    for shift in range(1, groups):
        most = jnp.maximum(most, lax.ppermute(count, "grp", [(g, (g + shift) % groups) for g in range(groups)]))
    blocks = tuple((b.reshape(rounds * HALVES, slab, rows, width) for b in (keys, values, queries)))
    sizes = sorted({slab, slab + slab // 4, slab + slab // 2, 2 * slab})
    dtype = keys.dtype

    def variant(number, cross):
        piece = lambda count: [pltpu.VMEM((count, rows, width), dtype) for _ in range(chunks)]
        dma = pltpu.SemaphoreType.DMA
        call = pl.pallas_call(
            lambda *refs: route_kernel(slab, chunks, cross, *refs),
            out_shape=[jax.ShapeDtypeStruct((HALVES, slab, rows, width), dtype)] * (chunks // HALVES),
            in_specs=[pl.BlockSpec(memory_space=pltpu.SMEM)] * 3 + [pl.BlockSpec(memory_space=pl.ANY)] * 3,
            out_specs=[pl.BlockSpec(memory_space=pl.ANY)] * (chunks // HALVES),
            scratch_shapes=piece(2 * slab) + piece(cross) + piece(cross) + piece(slab) + piece(slab)
            + [dma((chunks,)), dma((chunks,))]
            + [dma((chunks, slab - 1))] * 2 + [dma((chunks,))] * 6 + [dma((chunks, slab - 1))] * 2,
            compiler_params=pltpu.CompilerParams(collective_id=number, has_side_effects=True, vmem_limit_bytes=58 << 20),
            name=f"route_{cross}",
        )
        return lambda *operands: call(*operands)

    which = sum(((most > size).astype(jnp.int32) for size in sizes[:-1]))
    routed = lax.switch(which, [variant(n, size) for n, size in enumerate(sizes)], cross_idx, own_idx, outer_idx, *blocks)
    return [block.reshape(block_rows, width) for block in routed]


def body(state, keys, values, queries, rates, remaining, first_owner, migration):
    devices = lax.axis_size(("seq", "doc"))
    myself = lax.axis_index(("seq", "doc"))
    doc_first = inverse_of(first_owner)
    source_of = inverse_of(migration)
    weights = state[0]
    width = weights.shape[-1]
    block_rows = keys.shape[2]
    piece_rows = block_rows // devices

    def to_owners(section, doc_for_owner):
        blocks = (keys[section, 0], values[section, 0], queries[section, 0])
        split = tuple((member.reshape(devices, piece_rows, width) for member in blocks))
        dealt = move_rows(split)
        reordered = tuple((jnp.take(member, doc_for_owner, axis=0) for member in dealt))
        collected = move_rows(reordered)
        return tuple((member.reshape(block_rows, width) for member in collected))

    slab = devices // 4
    rounds = keys.shape[0]
    routed = None
    if devices % 4 == 0 and slab >= 4 and block_rows % (HALVES * slab * 16) == 0 and width % 128 == 0:
        routed = route_inputs(keys, values, queries, first_owner, doc_first)

    def run_round(section, weights_in, doc_for_owner):
        doc_here = doc_for_owner[myself]
        if routed is None:
            keys_here, values_here, queries_here = to_owners(section, doc_for_owner)
        else:
            keys_here, values_here, queries_here = routed[3 * section : 3 * section + 3]
        rate_here = lax.dynamic_index_in_dim(rates[section], doc_here, 0, keepdims=False)
        updated = fast_update(weights_in, keys_here, values_here, rate_here)
        return (updated, swiglu_apply(updated, queries_here), doc_here)

    updated, result_one, doc_one = run_round(0, weights, doc_first)
    outgoing = result_one.astype(jnp.bfloat16).reshape(devices, piece_rows, width)
    dealt_out = send_back(outgoing)
    returned = send_back(jnp.take(dealt_out, first_owner, axis=0))
    round_one = returned.reshape(1, block_rows, width)
    unused, result_two, doc_two = run_round(1, updated, doc_first)
    is_live = remaining[doc_two] >= 2
    masked = jnp.where(is_live, result_two, jnp.float32(0.0)).astype(jnp.bfloat16)
    dealt = move_result(masked.reshape(devices, piece_rows, width))
    regrouped = move_result(jnp.take(dealt, source_of, axis=0))
    round_two = regrouped.reshape(1, block_rows, width)
    return (round_one, round_two)


def solution(mesh):
    return jax.shard_map(
        body,
        mesh=mesh,
        in_specs=(
            P(("grp", "seq", "doc"), None, None, None),
            P(None, ("grp", "seq", "doc"), None, None),
            P(None, ("grp", "seq", "doc"), None, None),
            P(None, ("grp", "seq", "doc"), None, None),
            P(None, "grp", None),
            P("grp"),
            P("grp"),
            P("grp"),
        ),
        out_specs=(P(("grp", "seq", "doc"), None, None), P(("grp", "seq", "doc"), None, None)),
        check_vma=False,
    )
```

```python
import jax
import jax.numpy as jnp
from jax import lax
from jax.experimental import pallas as pl
from jax.experimental.pallas import tpu as pltpu
from jax.sharding import PartitionSpec as P

EPSILON = 1e-06
AXES = ("seq", "doc")
SPLIT_IN = 3
SPLIT_OUT = 6
AHEAD = 3


def shortened(array):

    def short(part):
        return part.astype(jnp.bfloat16) if part.dtype == jnp.float32 else part

    return jax.tree.map(short, array)


def swiglu_apply(weights, inputs):
    gate_pre = jnp.dot(inputs, weights[0], preferred_element_type=jnp.float32)
    upward = jnp.dot(inputs, weights[1], preferred_element_type=jnp.float32)
    hidden = (jax.nn.silu(gate_pre) * upward).astype(jnp.bfloat16)
    return jnp.dot(hidden, weights[2], preferred_element_type=jnp.float32)


def renorm(weight, gradient):
    before = weight.astype(jnp.float32)
    stepped = before - gradient
    factor = jnp.sqrt(jnp.mean(before * before, axis=0) + EPSILON) / jnp.sqrt(
        jnp.mean(stepped * stepped, axis=0) + EPSILON
    )
    return (stepped * factor[None, :]).astype(jnp.bfloat16)


def fast_update(weights, keys_rows, values_rows, rate_rows):
    gate_pre = jnp.dot(keys_rows, weights[0], preferred_element_type=jnp.float32)
    upward = jnp.dot(keys_rows, weights[1], preferred_element_type=jnp.float32)
    sigmoid_gate = jax.nn.sigmoid(gate_pre)
    active = gate_pre * sigmoid_gate
    hidden = (active * upward).astype(jnp.bfloat16)
    scaled_values = (rate_rows[:, None] * values_rows.astype(jnp.float32)).astype(jnp.bfloat16)
    grad_down = -jnp.dot(hidden.T, scaled_values, preferred_element_type=jnp.float32)
    grad_hidden = -jnp.dot(scaled_values, weights[2].T, preferred_element_type=jnp.float32)
    slope = sigmoid_gate * (1.0 + gate_pre * (1.0 - sigmoid_gate))
    grad_gate = (grad_hidden * upward * slope).astype(jnp.bfloat16)
    grad_up = (grad_hidden * active).astype(jnp.bfloat16)
    grad_first = jnp.dot(keys_rows.T, grad_gate, preferred_element_type=jnp.float32)
    grad_third = jnp.dot(keys_rows.T, grad_up, preferred_element_type=jnp.float32)
    return jnp.stack(
        [
            renorm(weights[0], grad_first),
            renorm(weights[1], grad_third),
            renorm(weights[2], grad_down),
        ]
    )


def inverse_of(permuted):
    count = permuted.shape[0]
    labels = jnp.arange(count, dtype=jnp.int32)
    return jnp.sum(jnp.where(permuted[None, :] == labels[:, None], labels[None, :], 0), axis=1)


def move_rows(items):
    return jax.tree.map(
        lambda part, own: part.astype(own.dtype),
        lax.all_to_all(shortened(items), ("seq", "doc"), split_axis=0, concat_axis=0, tiled=True),
        items,
    )


def send_back(pieces):
    return lax.all_to_all(pieces, ("seq", "doc"), split_axis=0, concat_axis=0, tiled=True)


def move_result(pieces):
    return lax.all_to_all(pieces, ("seq", "doc"), split_axis=0, concat_axis=0, tiled=True)


def route_kernel(slab, table, crosses, sources_n, outs_n, cross_idx, own_idx, outer_idx, *refs):
    chunks = len(table)
    sources, refs = refs[:sources_n], refs[sources_n:]
    outs, refs = refs[:outs_n], refs[outs_n:]
    held, refs = refs[:chunks], refs[chunks:]
    crossing, refs = refs[:chunks], refs[chunks:]
    crossed, refs = refs[:chunks], refs[chunks:]
    returning, refs = refs[:chunks], refs[chunks:]
    final, refs = refs[:chunks], refs[chunks:]
    local_in, local_out, deal_s, deal_r, in_s, in_r, mid_s, mid_r, back_s, back_r, last_s, last_r = refs
    cores = lax.axis_size("doc")
    me = lax.axis_index("seq") * cores + lax.axis_index("doc")
    here, member = me // slab, me % slab
    inner = (here == 1) | (here == 2)
    outer = (here == 0) | (here == 3)
    beside = here + 1 - 2 * (here % 2)
    opposite = 3 - here

    def device(which, who):
        index = which * slab + who
        return {"seq": index // cores, "doc": index % cores}

    def remote(src, dst, send, recv, target):
        return pltpu.make_async_remote_copy(
            src_ref=src, dst_ref=dst, send_sem=send, recv_sem=recv,
            device_id=target, device_id_type=pl.DeviceIdType.MESH,
        )

    def source(c):
        return sources[table[c][0]].at[table[c][1]]

    def deal(c):
        copies = []
        for r in range(1, slab):
            who = (member + r) % slab
            copies.append(remote(source(c).at[who], held[c].at[member], deal_s.at[c, r - 1], deal_r.at[c, r - 1], device(here, who)))
        return copies, pltpu.make_async_copy(source(c).at[member], held[c].at[member], local_in.at[c])

    def inward(c):
        return remote(held[c].at[pl.ds(0, slab)], held[c].at[pl.ds(slab, slab)], in_s.at[c], in_r.at[c], device(beside, member))

    def middle(c):
        return remote(crossing[c], crossed[c], mid_s.at[c], mid_r.at[c], device(opposite, member))

    def backward(c):
        return remote(returning[c], final[c], back_s.at[c], back_r.at[c], device(beside, member))

    def last(c):
        target = outs[table[c][2]].at[table[c][3]]
        copies = []
        for r in range(1, slab):
            who = (member + r) % slab
            copies.append(remote(final[c].at[who], target.at[member], last_s.at[c, r - 1], last_r.at[c, r - 1], device(here, who)))
        return copies, pltpu.make_async_copy(final[c].at[member], target.at[member], local_out.at[c])

    def start_all(group):
        for copy in group[0]:
            copy.start()
        group[1].start()

    barrier = pltpu.get_barrier_semaphore()
    for r in range(1, slab):
        pl.semaphore_signal(barrier, inc=1, device_id=device(here, (member + r) % slab), device_id_type=pl.DeviceIdType.MESH)
    pl.semaphore_signal(barrier, inc=1, device_id=device(beside, member), device_id_type=pl.DeviceIdType.MESH)

    @pl.when(inner)
    def _():
        pl.semaphore_signal(barrier, inc=1, device_id=device(opposite, member), device_id_type=pl.DeviceIdType.MESH)
        pl.semaphore_wait(barrier, slab + 1)

    @pl.when(outer)
    def _():
        pl.semaphore_wait(barrier, slab)

    for c in range(min(AHEAD, chunks)):
        start_all(deal(c))
    for t in range(chunks + 7):
        if t + AHEAD < chunks:
            start_all(deal(t + AHEAD))
        if t < chunks:
            copies, mine = deal(t)
            for copy in copies:
                copy.wait_recv()
            mine.wait()

        @pl.when(outer)
        def _():
            if t < chunks:
                inward(t).start()
            c = t - 7
            if 0 <= c < chunks:
                backward(c).wait_recv()
                start_all(last(c))

        @pl.when(inner)
        def _():
            c = t - 1
            if 0 <= c < chunks:
                inward(c).wait_recv()
                kind = table[c][4]

                def choose(j, carry):
                    crossing[c][j] = held[c][cross_idx[kind, j]]
                    return carry

                lax.fori_loop(0, crosses[kind], choose, 0)
                middle(c).start()
            c = t - 4
            if 0 <= c < chunks:
                middle(c).wait_recv()

                kind = table[c][4]

                def pick(index):
                    near = held[c][jnp.minimum(index, 2 * slab - 1)]
                    far = crossed[c][jnp.maximum(index - 2 * slab, 0)]
                    return jnp.where(index < 2 * slab, near, far)

                def give_back(j, carry):
                    returning[c][j] = pick(outer_idx[kind, j])
                    return carry

                def keep(j, carry):
                    final[c][j] = pick(own_idx[kind, j])
                    return carry

                lax.fori_loop(0, slab, give_back, 0)
                backward(c).start()
                lax.fori_loop(0, slab, keep, 0)
                start_all(last(c))

    for c in range(chunks):
        for copy in deal(c)[0]:
            copy.wait_send()
        copies, mine = last(c)
        for copy in copies:
            copy.wait_send()
            copy.wait_recv()
        mine.wait()

        @pl.when(outer)
        def _():
            inward(c).wait_send()

        @pl.when(inner)
        def _():
            middle(c).wait_send()
            backward(c).wait_send()


def plan(target, source):
    devices = target.shape[0]
    slab = devices // 4
    here = jnp.clip(lax.axis_index(AXES) // slab, 1, 2)
    outer = jnp.where(here == 1, 0, 3)
    ids = jnp.arange(devices, dtype=jnp.int32)
    low = ids < 2 * slab
    goes = low != (target < 2 * slab)
    order = jnp.where(low, (ids + slab) % (2 * slab), ids - 2 * slab)
    before = goes[None, :] & (low[None, :] == low[:, None]) & (order[None, :] < order[:, None])
    rank = jnp.sum(before.astype(jnp.int32), axis=1)
    mine = low == (here == 1)
    slot = jnp.where(mine, order, 2 * slab + rank)
    j = jnp.arange(2 * slab, dtype=jnp.int32)
    hit = goes[None, :] & mine[None, :] & (rank[None, :] == j[:, None])
    cross_idx = jnp.sum(jnp.where(hit, order[None, :], 0), axis=1).astype(jnp.int32)
    is_source = source[:, None] == ids[None, :]
    owner_slot = jnp.sum(jnp.where(is_source, slot[None, :], 0), axis=1).astype(jnp.int32)
    own_idx = lax.dynamic_slice(owner_slot, (here * slab,), (slab,))
    outer_idx = lax.dynamic_slice(owner_slot, (outer * slab,), (slab,))
    return cross_idx, own_idx, outer_idx


def crossing_class(first_owner, sizes):
    devices = first_owner.shape[0]
    low = jnp.arange(devices, dtype=jnp.int32) < devices // 2
    count = jnp.sum((low & (first_owner >= devices // 2)).astype(jnp.int32))
    groups = lax.axis_size("grp")
    most = count
    for shift in range(1, groups):
        most = jnp.maximum(most, lax.ppermute(count, "grp", [(g, (g + shift) % groups) for g in range(groups)]))
    return sum(((most > size).astype(jnp.int32) for size in sizes[:-1]))


def route(base, which, sizes, fixed, plans, operands, table, outs_n, split, slab):
    rows, width = operands[0].shape[2:]
    dtype = operands[0].dtype
    chunks = len(table)
    indices = [jnp.stack(members) for members in zip(*plans)]

    def variant(number, cross):
        crosses = (cross,) + fixed
        piece = lambda count: [pltpu.VMEM((count, rows, width), dtype) for _ in range(chunks)]
        mids = lambda: [pltpu.VMEM((crosses[entry[4]], rows, width), dtype) for entry in table]
        dma = pltpu.SemaphoreType.DMA
        call = pl.pallas_call(
            lambda *refs: route_kernel(slab, table, crosses, len(operands), outs_n, *refs),
            out_shape=[jax.ShapeDtypeStruct((split, slab, rows, width), dtype)] * outs_n,
            in_specs=[pl.BlockSpec(memory_space=pltpu.SMEM)] * 3 + [pl.BlockSpec(memory_space=pl.ANY)] * len(operands),
            out_specs=[pl.BlockSpec(memory_space=pl.ANY)] * outs_n,
            scratch_shapes=piece(2 * slab) + mids() + mids() + piece(slab) + piece(slab)
            + [dma((chunks,)), dma((chunks,))]
            + [dma((chunks, slab - 1))] * 2 + [dma((chunks,))] * 6 + [dma((chunks, slab - 1))] * 2,
            compiler_params=pltpu.CompilerParams(collective_id=number, has_side_effects=True, vmem_limit_bytes=58 << 20),
            name=f"route_{base}_{cross}",
        )
        return lambda *args: call(*args)

    return lax.switch(which, [variant(base + n, size) for n, size in enumerate(sizes)], *indices, *operands)


def body(state, keys, values, queries, rates, remaining, first_owner, migration):
    devices = lax.axis_size(("seq", "doc"))
    myself = lax.axis_index(("seq", "doc"))
    doc_first = inverse_of(first_owner)
    source_of = inverse_of(migration)
    weights = state[0]
    width = weights.shape[-1]
    block_rows = keys.shape[2]
    piece_rows = block_rows // devices

    def to_owners(section, doc_for_owner):
        blocks = (keys[section, 0], values[section, 0], queries[section, 0])
        split = tuple((member.reshape(devices, piece_rows, width) for member in blocks))
        dealt = move_rows(split)
        reordered = tuple((jnp.take(member, doc_for_owner, axis=0) for member in dealt))
        collected = move_rows(reordered)
        return tuple((member.reshape(block_rows, width) for member in collected))

    slab = devices // 4
    rounds = keys.shape[0]
    routed = None
    finest = SPLIT_OUT * slab * 16
    if devices % 4 == 0 and slab >= 4 and block_rows % finest == 0 and width % 128 == 0:
        sizes = sorted({slab, slab + slab // 4, slab + slab // 2, 2 * slab})
        which = crossing_class(first_owner, sizes)
        cut = lambda block, count, split: block.reshape(count * split, slab, block_rows // (split * slab), width)
        table = [
            (tensor, section * SPLIT_IN + part, section * 3 + tensor, part, 0)
            for section in range(rounds)
            for tensor in range(3)
            for part in range(SPLIT_IN)
        ]
        operands = [cut(block, rounds, SPLIT_IN) for block in (keys, values, queries)]
        routed = route(0, which, sizes, (), [plan(first_owner, doc_first)], operands, table, 3 * rounds, SPLIT_IN, slab)
        routed = [block.reshape(block_rows, width) for block in routed]

    def run_round(section, weights_in, doc_for_owner):
        doc_here = doc_for_owner[myself]
        if routed is None:
            keys_here, values_here, queries_here = to_owners(section, doc_for_owner)
        else:
            keys_here, values_here, queries_here = routed[3 * section : 3 * section + 3]
        rate_here = lax.dynamic_index_in_dim(rates[section], doc_here, 0, keepdims=False)
        updated = fast_update(weights_in, keys_here, values_here, rate_here)
        return (updated, swiglu_apply(updated, queries_here), doc_here)

    updated, result_one, doc_one = run_round(0, weights, doc_first)
    outgoing = result_one.astype(jnp.bfloat16)
    if routed is None:
        dealt_out = send_back(outgoing.reshape(devices, piece_rows, width))
        returned = send_back(jnp.take(dealt_out, first_owner, axis=0))
        round_one = returned.reshape(1, block_rows, width)
    unused, result_two, doc_two = run_round(1, updated, doc_first)
    is_live = remaining[doc_two] >= 2
    masked = jnp.where(is_live, result_two, jnp.float32(0.0)).astype(jnp.bfloat16)
    if routed is None:
        dealt = move_result(masked.reshape(devices, piece_rows, width))
        regrouped = move_result(jnp.take(dealt, source_of, axis=0))
        round_two = regrouped.reshape(1, block_rows, width)
    else:
        table = [(tensor, part, tensor, part, tensor) for part in range(SPLIT_OUT) for tensor in range(2)]
        plans = [plan(doc_first, first_owner), plan(migration, source_of)]
        operands = [cut(block, 1, SPLIT_OUT) for block in (outgoing, masked)]
        moving = devices // 8
        sent = route(len(sizes), which // 2, sizes[1::2], (moving,), plans, operands, table, 2, SPLIT_OUT, slab)
        round_one, round_two = (block.reshape(1, block_rows, width) for block in sent)
    return (round_one, round_two)


def solution(mesh):
    return jax.shard_map(
        body,
        mesh=mesh,
        in_specs=(
            P(("grp", "seq", "doc"), None, None, None),
            P(None, ("grp", "seq", "doc"), None, None),
            P(None, ("grp", "seq", "doc"), None, None),
            P(None, ("grp", "seq", "doc"), None, None),
            P(None, "grp", None),
            P("grp"),
            P("grp"),
            P("grp"),
        ),
        out_specs=(P(("grp", "seq", "doc"), None, None), P(("grp", "seq", "doc"), None, None)),
        check_vma=False,
    )
```

```python
import jax
import jax.numpy as jnp
from jax import lax
from jax.experimental import pallas as pl
from jax.experimental.pallas import tpu as pltpu
from jax.sharding import PartitionSpec as P

EPSILON = 1e-06
AXES = ("seq", "doc")
SPLIT_IN = 2
SPLIT_OUT = 6
AHEAD = 3


def shortened(array):

    def short(part):
        return part.astype(jnp.bfloat16) if part.dtype == jnp.float32 else part

    return jax.tree.map(short, array)


def swiglu_apply(weights, inputs):
    gate_pre = jnp.dot(inputs, weights[0], preferred_element_type=jnp.float32)
    upward = jnp.dot(inputs, weights[1], preferred_element_type=jnp.float32)
    hidden = (jax.nn.silu(gate_pre) * upward).astype(jnp.bfloat16)
    return jnp.dot(hidden, weights[2], preferred_element_type=jnp.float32)


def renorm(weight, gradient):
    before = weight.astype(jnp.float32)
    stepped = before - gradient
    factor = jnp.sqrt(jnp.mean(before * before, axis=0) + EPSILON) / jnp.sqrt(
        jnp.mean(stepped * stepped, axis=0) + EPSILON
    )
    return (stepped * factor[None, :]).astype(jnp.bfloat16)


def fast_update(weights, keys_rows, values_rows, rate_rows):
    gate_pre = jnp.dot(keys_rows, weights[0], preferred_element_type=jnp.float32)
    upward = jnp.dot(keys_rows, weights[1], preferred_element_type=jnp.float32)
    sigmoid_gate = jax.nn.sigmoid(gate_pre)
    active = gate_pre * sigmoid_gate
    hidden = (active * upward).astype(jnp.bfloat16)
    scaled_values = (rate_rows[:, None] * values_rows.astype(jnp.float32)).astype(jnp.bfloat16)
    grad_down = -jnp.dot(hidden.T, scaled_values, preferred_element_type=jnp.float32)
    grad_hidden = -jnp.dot(scaled_values, weights[2].T, preferred_element_type=jnp.float32)
    slope = sigmoid_gate * (1.0 + gate_pre * (1.0 - sigmoid_gate))
    grad_gate = (grad_hidden * upward * slope).astype(jnp.bfloat16)
    grad_up = (grad_hidden * active).astype(jnp.bfloat16)
    grad_first = jnp.dot(keys_rows.T, grad_gate, preferred_element_type=jnp.float32)
    grad_third = jnp.dot(keys_rows.T, grad_up, preferred_element_type=jnp.float32)
    return jnp.stack(
        [
            renorm(weights[0], grad_first),
            renorm(weights[1], grad_third),
            renorm(weights[2], grad_down),
        ]
    )


def inverse_of(permuted):
    count = permuted.shape[0]
    labels = jnp.arange(count, dtype=jnp.int32)
    return jnp.sum(jnp.where(permuted[None, :] == labels[:, None], labels[None, :], 0), axis=1)


def move_rows(items):
    return jax.tree.map(
        lambda part, own: part.astype(own.dtype),
        lax.all_to_all(shortened(items), ("seq", "doc"), split_axis=0, concat_axis=0, tiled=True),
        items,
    )


def send_back(pieces):
    return lax.all_to_all(pieces, ("seq", "doc"), split_axis=0, concat_axis=0, tiled=True)


def move_result(pieces):
    return lax.all_to_all(pieces, ("seq", "doc"), split_axis=0, concat_axis=0, tiled=True)


def route_kernel(slab, table, crosses, sources_n, outs_n, cross_idx, owner_idx, *refs):
    chunks = len(table)
    sources, refs = refs[:sources_n], refs[sources_n:]
    outs, refs = refs[:outs_n], refs[outs_n:]
    held, refs = refs[:chunks], refs[chunks:]
    crossing, refs = refs[:chunks], refs[chunks:]
    crossed, refs = refs[:chunks], refs[chunks:]
    sorted_by, refs = refs[:chunks], refs[chunks:]
    returning = [ref.at[pl.ds(0, slab)] for ref in sorted_by]
    final = [ref.at[pl.ds(slab, slab)] for ref in sorted_by]
    local_in, local_out, deal_s, deal_r, in_s, in_r, mid_s, mid_r, back_s, back_r, last_s, last_r = refs
    cores = lax.axis_size("doc")
    me = lax.axis_index("seq") * cores + lax.axis_index("doc")
    here, member = me // slab, me % slab
    inner = (here == 1) | (here == 2)
    outer = (here == 0) | (here == 3)
    beside = here + 1 - 2 * (here % 2)
    opposite = 3 - here

    def device(which, who):
        index = which * slab + who
        return {"seq": index // cores, "doc": index % cores}

    def remote(src, dst, send, recv, target):
        return pltpu.make_async_remote_copy(
            src_ref=src, dst_ref=dst, send_sem=send, recv_sem=recv,
            device_id=target, device_id_type=pl.DeviceIdType.MESH,
        )

    def source(c):
        return sources[table[c][0]].at[table[c][1]]

    def deal(c):
        copies = []
        for r in range(1, slab):
            who = (member + r) % slab
            copies.append(remote(source(c).at[who], held[c].at[member], deal_s.at[c], deal_r.at[c], device(here, who)))
        return copies, pltpu.make_async_copy(source(c).at[member], held[c].at[member], local_in.at[c])

    def dealt(c):
        whole = held[c].at[pl.ds(0, slab - 1)]
        return remote(whole, whole, deal_s.at[c], deal_r.at[c], device(here, (member + 1) % slab))

    def lasting(c):
        whole = final[c].at[pl.ds(0, slab - 1)]
        return remote(whole, whole, last_s.at[c], last_r.at[c], device(here, (member + 1) % slab))

    def inward(c):
        return remote(held[c].at[pl.ds(0, slab)], held[c].at[pl.ds(slab, slab)], in_s.at[c], in_r.at[c], device(beside, member))

    def middle(c):
        return remote(crossing[c], crossed[c], mid_s.at[c], mid_r.at[c], device(opposite, member))

    def backward(c):
        return remote(returning[c], final[c], back_s.at[c], back_r.at[c], device(beside, member))

    def last(c):
        target = outs[table[c][2]].at[table[c][3]]
        copies = []
        for r in range(1, slab):
            who = (member + r) % slab
            copies.append(remote(final[c].at[who], target.at[member], last_s.at[c], last_r.at[c], device(here, who)))
        return copies, pltpu.make_async_copy(final[c].at[member], target.at[member], local_out.at[c])

    def start_all(group):
        for copy in group[0]:
            copy.start()
        group[1].start()

    barrier = pltpu.get_barrier_semaphore()
    for r in range(1, slab):
        pl.semaphore_signal(barrier, inc=1, device_id=device(here, (member + r) % slab), device_id_type=pl.DeviceIdType.MESH)
    pl.semaphore_signal(barrier, inc=1, device_id=device(beside, member), device_id_type=pl.DeviceIdType.MESH)

    @pl.when(inner)
    def _():
        pl.semaphore_signal(barrier, inc=1, device_id=device(opposite, member), device_id_type=pl.DeviceIdType.MESH)
        pl.semaphore_wait(barrier, slab + 1)

    @pl.when(outer)
    def _():
        pl.semaphore_wait(barrier, slab)

    for c in range(min(AHEAD, chunks)):
        start_all(deal(c))
    for t in range(chunks + 7):
        if t + AHEAD < chunks:
            start_all(deal(t + AHEAD))
        if t < chunks:
            dealt(t).wait_recv()
            deal(t)[1].wait()

        @pl.when(outer)
        def _():
            if t < chunks:
                inward(t).start()
            c = t - 7
            if 0 <= c < chunks:
                backward(c).wait_recv()
                start_all(last(c))

        @pl.when(inner)
        def _():
            c = t - 1
            if 0 <= c < chunks:
                inward(c).wait_recv()
                kind = table[c][4]

                def choose(j, carry):
                    crossing[c][j] = held[c][cross_idx[kind, j]]
                    return carry

                lax.fori_loop(0, crosses[kind], choose, 0)
                middle(c).start()
            c = t - 4
            if 0 <= c < chunks:
                middle(c).wait_recv()

                kind = table[c][4]

                def pick(index):
                    near = held[c][jnp.minimum(index, 2 * slab - 1)]
                    far = crossed[c][jnp.maximum(index - 2 * slab, 0)]
                    return jnp.where(index < 2 * slab, near, far)

                def place(j, carry):
                    sorted_by[c][j] = pick(owner_idx[kind, j])
                    return carry

                lax.fori_loop(0, 2 * slab, place, 0)
                backward(c).start()
                start_all(last(c))

    for c in range(chunks):
        dealt(c).wait_send()
        lasting(c).wait()
        last(c)[1].wait()

        @pl.when(outer)
        def _():
            inward(c).wait_send()

        @pl.when(inner)
        def _():
            middle(c).wait_send()
            backward(c).wait_send()


def plan(target, source):
    devices = target.shape[0]
    slab = devices // 4
    here = jnp.clip(lax.axis_index(AXES) // slab, 1, 2)
    outer = jnp.where(here == 1, 0, 3)
    ids = jnp.arange(devices, dtype=jnp.int32)
    low = ids < 2 * slab
    goes = low != (target < 2 * slab)
    order = jnp.where(low, (ids + slab) % (2 * slab), ids - 2 * slab)
    before = goes[None, :] & (low[None, :] == low[:, None]) & (order[None, :] < order[:, None])
    rank = jnp.sum(before.astype(jnp.int32), axis=1)
    mine = low == (here == 1)
    slot = jnp.where(mine, order, 2 * slab + rank)
    j = jnp.arange(2 * slab, dtype=jnp.int32)
    hit = goes[None, :] & mine[None, :] & (rank[None, :] == j[:, None])
    cross_idx = jnp.sum(jnp.where(hit, order[None, :], 0), axis=1).astype(jnp.int32)
    is_source = source[:, None] == ids[None, :]
    owner_slot = jnp.sum(jnp.where(is_source, slot[None, :], 0), axis=1).astype(jnp.int32)
    own_idx = lax.dynamic_slice(owner_slot, (here * slab,), (slab,))
    outer_idx = lax.dynamic_slice(owner_slot, (outer * slab,), (slab,))
    return cross_idx, jnp.concatenate([outer_idx, own_idx])


def crossing_class(first_owner, sizes):
    devices = first_owner.shape[0]
    low = jnp.arange(devices, dtype=jnp.int32) < devices // 2
    count = jnp.sum((low & (first_owner >= devices // 2)).astype(jnp.int32))
    groups = lax.axis_size("grp")
    most = count
    for shift in range(1, groups):
        most = jnp.maximum(most, lax.ppermute(count, "grp", [(g, (g + shift) % groups) for g in range(groups)]))
    return sum(((most > size).astype(jnp.int32) for size in sizes[:-1]))


def route(base, which, sizes, fixed, plans, operands, table, outs_n, split, slab):
    rows, width = operands[0].shape[2:]
    dtype = operands[0].dtype
    chunks = len(table)
    indices = [jnp.stack(members) for members in zip(*plans)]

    def variant(number, cross):
        crosses = (cross,) + fixed
        piece = lambda count: [pltpu.VMEM((count, rows, width), dtype) for _ in range(chunks)]
        mids = lambda: [pltpu.VMEM((crosses[entry[4]], rows, width), dtype) for entry in table]
        dma = pltpu.SemaphoreType.DMA
        call = pl.pallas_call(
            lambda *refs: route_kernel(slab, table, crosses, len(operands), outs_n, *refs),
            out_shape=[jax.ShapeDtypeStruct((split, slab, rows, width), dtype)] * outs_n,
            in_specs=[pl.BlockSpec(memory_space=pltpu.SMEM)] * 2 + [pl.BlockSpec(memory_space=pl.ANY)] * len(operands),
            out_specs=[pl.BlockSpec(memory_space=pl.ANY)] * outs_n,
            scratch_shapes=piece(2 * slab) + mids() + mids() + piece(2 * slab)
            + [dma((chunks,)), dma((chunks,))]
            + [dma((chunks,))] * 10,
            compiler_params=pltpu.CompilerParams(collective_id=number, has_side_effects=True, vmem_limit_bytes=58 << 20),
            name=f"route_{base}_{cross}",
        )
        return lambda *args: call(*args)

    return lax.switch(which, [variant(base + n, size) for n, size in enumerate(sizes)], *indices, *operands)


def body(state, keys, values, queries, rates, remaining, first_owner, migration):
    devices = lax.axis_size(("seq", "doc"))
    myself = lax.axis_index(("seq", "doc"))
    doc_first = inverse_of(first_owner)
    source_of = inverse_of(migration)
    weights = state[0]
    width = weights.shape[-1]
    block_rows = keys.shape[2]
    piece_rows = block_rows // devices

    def to_owners(section, doc_for_owner):
        blocks = (keys[section, 0], values[section, 0], queries[section, 0])
        split = tuple((member.reshape(devices, piece_rows, width) for member in blocks))
        dealt = move_rows(split)
        reordered = tuple((jnp.take(member, doc_for_owner, axis=0) for member in dealt))
        collected = move_rows(reordered)
        return tuple((member.reshape(block_rows, width) for member in collected))

    slab = devices // 4
    rounds = keys.shape[0]
    routed = None
    finest = SPLIT_OUT * slab * 16
    if devices % 4 == 0 and slab >= 4 and block_rows % finest == 0 and width % 128 == 0:
        sizes = sorted({slab, slab + slab // 4, slab + slab // 2, 2 * slab})
        which = crossing_class(first_owner, sizes)
        cut = lambda block, count, split: block.reshape(count * split, slab, block_rows // (split * slab), width)
        table = [
            (tensor, section * SPLIT_IN + part, section * 3 + tensor, part, 0)
            for section in range(rounds)
            for tensor in range(3)
            for part in range(SPLIT_IN)
        ]
        operands = [cut(block, rounds, SPLIT_IN) for block in (keys, values, queries)]
        routed = route(0, which, sizes, (), [plan(first_owner, doc_first)], operands, table, 3 * rounds, SPLIT_IN, slab)
        routed = [block.reshape(block_rows, width) for block in routed]

    def run_round(section, weights_in, doc_for_owner):
        doc_here = doc_for_owner[myself]
        if routed is None:
            keys_here, values_here, queries_here = to_owners(section, doc_for_owner)
        else:
            keys_here, values_here, queries_here = routed[3 * section : 3 * section + 3]
        rate_here = lax.dynamic_index_in_dim(rates[section], doc_here, 0, keepdims=False)
        updated = fast_update(weights_in, keys_here, values_here, rate_here)
        return (updated, swiglu_apply(updated, queries_here), doc_here)

    updated, result_one, doc_one = run_round(0, weights, doc_first)
    outgoing = result_one.astype(jnp.bfloat16)
    if routed is None:
        dealt_out = send_back(outgoing.reshape(devices, piece_rows, width))
        returned = send_back(jnp.take(dealt_out, first_owner, axis=0))
        round_one = returned.reshape(1, block_rows, width)
    unused, result_two, doc_two = run_round(1, updated, doc_first)
    is_live = remaining[doc_two] >= 2
    masked = jnp.where(is_live, result_two, jnp.float32(0.0)).astype(jnp.bfloat16)
    if routed is None:
        dealt = move_result(masked.reshape(devices, piece_rows, width))
        regrouped = move_result(jnp.take(dealt, source_of, axis=0))
        round_two = regrouped.reshape(1, block_rows, width)
    else:
        table = [(tensor, part, tensor, part, tensor) for part in range(SPLIT_OUT) for tensor in range(2)]
        plans = [plan(doc_first, first_owner), plan(migration, source_of)]
        operands = [cut(block, 1, SPLIT_OUT) for block in (outgoing, masked)]
        moving = devices // 8
        sent = route(len(sizes), which // 2, sizes[1::2], (moving,), plans, operands, table, 2, SPLIT_OUT, slab)
        round_one, round_two = (block.reshape(1, block_rows, width) for block in sent)
    return (round_one, round_two)


def solution(mesh):
    return jax.shard_map(
        body,
        mesh=mesh,
        in_specs=(
            P(("grp", "seq", "doc"), None, None, None),
            P(None, ("grp", "seq", "doc"), None, None),
            P(None, ("grp", "seq", "doc"), None, None),
            P(None, ("grp", "seq", "doc"), None, None),
            P(None, "grp", None),
            P("grp"),
            P("grp"),
            P("grp"),
        ),
        out_specs=(P(("grp", "seq", "doc"), None, None), P(("grp", "seq", "doc"), None, None)),
        check_vma=False,
    )
```

```python
import jax
import jax.numpy as jnp
from jax import lax
from jax.experimental import pallas as pl
from jax.experimental.pallas import tpu as pltpu
from jax.sharding import PartitionSpec as P

EPSILON = 1e-06
AXES = ("seq", "doc")
SPLIT_IN = 2
SPLIT_OUT = 6
AHEAD = 2


def shortened(array):

    def short(part):
        return part.astype(jnp.bfloat16) if part.dtype == jnp.float32 else part

    return jax.tree.map(short, array)


def swiglu_apply(weights, inputs):
    gate_pre = jnp.dot(inputs, weights[0], preferred_element_type=jnp.float32)
    upward = jnp.dot(inputs, weights[1], preferred_element_type=jnp.float32)
    hidden = (jax.nn.silu(gate_pre) * upward).astype(jnp.bfloat16)
    return jnp.dot(hidden, weights[2], preferred_element_type=jnp.float32)


def renorm(weight, gradient):
    before = weight.astype(jnp.float32)
    stepped = before - gradient
    factor = jnp.sqrt(jnp.mean(before * before, axis=0) + EPSILON) / jnp.sqrt(
        jnp.mean(stepped * stepped, axis=0) + EPSILON
    )
    return (stepped * factor[None, :]).astype(jnp.bfloat16)


def fast_update(weights, keys_rows, values_rows, rate_rows):
    gate_pre = jnp.dot(keys_rows, weights[0], preferred_element_type=jnp.float32)
    upward = jnp.dot(keys_rows, weights[1], preferred_element_type=jnp.float32)
    sigmoid_gate = jax.nn.sigmoid(gate_pre)
    active = gate_pre * sigmoid_gate
    hidden = (active * upward).astype(jnp.bfloat16)
    scaled_values = (rate_rows[:, None] * values_rows.astype(jnp.float32)).astype(jnp.bfloat16)
    grad_down = -jnp.dot(hidden.T, scaled_values, preferred_element_type=jnp.float32)
    grad_hidden = -jnp.dot(scaled_values, weights[2].T, preferred_element_type=jnp.float32)
    slope = sigmoid_gate * (1.0 + gate_pre * (1.0 - sigmoid_gate))
    grad_gate = (grad_hidden * upward * slope).astype(jnp.bfloat16)
    grad_up = (grad_hidden * active).astype(jnp.bfloat16)
    grad_first = jnp.dot(keys_rows.T, grad_gate, preferred_element_type=jnp.float32)
    grad_third = jnp.dot(keys_rows.T, grad_up, preferred_element_type=jnp.float32)
    return jnp.stack(
        [
            renorm(weights[0], grad_first),
            renorm(weights[1], grad_third),
            renorm(weights[2], grad_down),
        ]
    )


def inverse_of(permuted):
    count = permuted.shape[0]
    labels = jnp.arange(count, dtype=jnp.int32)
    return jnp.sum(jnp.where(permuted[None, :] == labels[:, None], labels[None, :], 0), axis=1)


def move_rows(items):
    return jax.tree.map(
        lambda part, own: part.astype(own.dtype),
        lax.all_to_all(shortened(items), ("seq", "doc"), split_axis=0, concat_axis=0, tiled=True),
        items,
    )


def send_back(pieces):
    return lax.all_to_all(pieces, ("seq", "doc"), split_axis=0, concat_axis=0, tiled=True)


def move_result(pieces):
    return lax.all_to_all(pieces, ("seq", "doc"), split_axis=0, concat_axis=0, tiled=True)


def route_kernel(slab, table, crosses, sources_n, outs_n, cross_idx, owner_idx, *refs):
    chunks = len(table)
    sources, refs = refs[:sources_n], refs[sources_n:]
    outs, refs = refs[:outs_n], refs[outs_n:]
    held, refs = refs[:chunks], refs[chunks:]
    crossing, refs = refs[:chunks], refs[chunks:]
    crossed, refs = refs[:chunks], refs[chunks:]
    sorted_by, refs = refs[:chunks], refs[chunks:]
    returning = [ref.at[pl.ds(0, slab)] for ref in sorted_by]
    final = [ref.at[pl.ds(slab, slab)] for ref in sorted_by]
    local_in, local_out, deal_s, deal_r, in_s, in_r, mid_s, mid_r, back_s, back_r, last_s, last_r = refs
    cores = lax.axis_size("doc")
    me = lax.axis_index("seq") * cores + lax.axis_index("doc")
    here, member = me // slab, me % slab
    inner = (here == 1) | (here == 2)
    outer = (here == 0) | (here == 3)
    beside = here + 1 - 2 * (here % 2)
    opposite = 3 - here

    def device(which, who):
        index = which * slab + who
        return {"seq": index // cores, "doc": index % cores}

    def remote(src, dst, send, recv, target):
        return pltpu.make_async_remote_copy(
            src_ref=src, dst_ref=dst, send_sem=send, recv_sem=recv,
            device_id=target, device_id_type=pl.DeviceIdType.MESH,
        )

    def source(c):
        return sources[table[c][0]].at[table[c][1]]

    def deal(c):
        copies = []
        for r in range(1, slab):
            who = (member + r) % slab
            copies.append(remote(source(c).at[who], held[c].at[member], deal_s.at[c], deal_r.at[c], device(here, who)))
        return copies, pltpu.make_async_copy(source(c).at[member], held[c].at[member], local_in.at[c])

    def dealt(c):
        whole = held[c].at[pl.ds(0, slab - 1)]
        return remote(whole, whole, deal_s.at[c], deal_r.at[c], device(here, (member + 1) % slab))

    def lasting(c):
        whole = final[c].at[pl.ds(0, slab - 1)]
        return remote(whole, whole, last_s.at[c], last_r.at[c], device(here, (member + 1) % slab))

    def inward(c):
        return remote(held[c].at[pl.ds(0, slab)], held[c].at[pl.ds(slab, slab)], in_s.at[c], in_r.at[c], device(beside, member))

    def middle(c):
        return remote(crossing[c], crossed[c], mid_s.at[c], mid_r.at[c], device(opposite, member))

    def backward(c):
        return remote(returning[c], final[c], back_s.at[c], back_r.at[c], device(beside, member))

    def last(c):
        target = outs[table[c][2]].at[table[c][3]]
        copies = []
        for r in range(1, slab):
            who = (member + r) % slab
            copies.append(remote(final[c].at[who], target.at[member], last_s.at[c], last_r.at[c], device(here, who)))
        return copies, pltpu.make_async_copy(final[c].at[member], target.at[member], local_out.at[c])

    def start_all(group):
        for copy in group[0]:
            copy.start()
        group[1].start()

    barrier = pltpu.get_barrier_semaphore()
    for r in range(1, slab):
        pl.semaphore_signal(barrier, inc=1, device_id=device(here, (member + r) % slab), device_id_type=pl.DeviceIdType.MESH)
    pl.semaphore_signal(barrier, inc=1, device_id=device(beside, member), device_id_type=pl.DeviceIdType.MESH)

    @pl.when(inner)
    def _():
        pl.semaphore_signal(barrier, inc=1, device_id=device(opposite, member), device_id_type=pl.DeviceIdType.MESH)
        pl.semaphore_wait(barrier, slab + 1)

    @pl.when(outer)
    def _():
        pl.semaphore_wait(barrier, slab)

    for c in range(min(AHEAD, chunks)):
        start_all(deal(c))
    for t in range(chunks + 7):
        for c in range(AHEAD + 2 * t, min(AHEAD + 2 * t + 2, chunks)):
            start_all(deal(c))
        if t < chunks:
            dealt(t).wait_recv()
            deal(t)[1].wait()

        @pl.when(outer)
        def _():
            if t < chunks:
                inward(t).start()
            c = t - 7
            if 0 <= c < chunks:
                backward(c).wait_recv()
                start_all(last(c))

        @pl.when(inner)
        def _():
            c = t - 1
            if 0 <= c < chunks:
                inward(c).wait_recv()
                kind = table[c][4]

                def choose(j, carry):
                    crossing[c][j] = held[c][cross_idx[kind, j]]
                    return carry

                lax.fori_loop(0, crosses[kind], choose, 0)
                middle(c).start()
            c = t - 4
            if 0 <= c < chunks:
                middle(c).wait_recv()

                kind = table[c][4]

                def pick(index):
                    near = held[c][jnp.minimum(index, 2 * slab - 1)]
                    far = crossed[c][jnp.maximum(index - 2 * slab, 0)]
                    return jnp.where(index < 2 * slab, near, far)

                def place(j, carry):
                    sorted_by[c][j] = pick(owner_idx[kind, j])
                    return carry

                lax.fori_loop(0, 2 * slab, place, 0)
                backward(c).start()
                start_all(last(c))

    for c in range(chunks):
        dealt(c).wait_send()
        lasting(c).wait()
        last(c)[1].wait()

        @pl.when(outer)
        def _():
            inward(c).wait_send()

        @pl.when(inner)
        def _():
            middle(c).wait_send()
            backward(c).wait_send()


def plan(target, source):
    devices = target.shape[0]
    slab = devices // 4
    here = jnp.clip(lax.axis_index(AXES) // slab, 1, 2)
    outer = jnp.where(here == 1, 0, 3)
    ids = jnp.arange(devices, dtype=jnp.int32)
    low = ids < 2 * slab
    goes = low != (target < 2 * slab)
    order = jnp.where(low, (ids + slab) % (2 * slab), ids - 2 * slab)
    before = goes[None, :] & (low[None, :] == low[:, None]) & (order[None, :] < order[:, None])
    rank = jnp.sum(before.astype(jnp.int32), axis=1)
    mine = low == (here == 1)
    slot = jnp.where(mine, order, 2 * slab + rank)
    j = jnp.arange(2 * slab, dtype=jnp.int32)
    hit = goes[None, :] & mine[None, :] & (rank[None, :] == j[:, None])
    cross_idx = jnp.sum(jnp.where(hit, order[None, :], 0), axis=1).astype(jnp.int32)
    is_source = source[:, None] == ids[None, :]
    owner_slot = jnp.sum(jnp.where(is_source, slot[None, :], 0), axis=1).astype(jnp.int32)
    own_idx = lax.dynamic_slice(owner_slot, (here * slab,), (slab,))
    outer_idx = lax.dynamic_slice(owner_slot, (outer * slab,), (slab,))
    return cross_idx, jnp.concatenate([outer_idx, own_idx])


def crossing_class(first_owner, sizes):
    devices = first_owner.shape[0]
    low = jnp.arange(devices, dtype=jnp.int32) < devices // 2
    count = jnp.sum((low & (first_owner >= devices // 2)).astype(jnp.int32))
    groups = lax.axis_size("grp")
    most = count
    for shift in range(1, groups):
        most = jnp.maximum(most, lax.ppermute(count, "grp", [(g, (g + shift) % groups) for g in range(groups)]))
    return sum(((most > size).astype(jnp.int32) for size in sizes[:-1]))


def route(base, which, sizes, fixed, plans, operands, table, outs_n, split, slab):
    rows, width = operands[0].shape[2:]
    dtype = operands[0].dtype
    chunks = len(table)
    indices = [jnp.stack(members) for members in zip(*plans)]

    def variant(number, cross):
        crosses = (cross,) + fixed
        piece = lambda count: [pltpu.VMEM((count, rows, width), dtype) for _ in range(chunks)]
        mids = lambda: [pltpu.VMEM((crosses[entry[4]], rows, width), dtype) for entry in table]
        dma = pltpu.SemaphoreType.DMA
        call = pl.pallas_call(
            lambda *refs: route_kernel(slab, table, crosses, len(operands), outs_n, *refs),
            out_shape=[jax.ShapeDtypeStruct((split, slab, rows, width), dtype)] * outs_n,
            in_specs=[pl.BlockSpec(memory_space=pltpu.SMEM)] * 2 + [pl.BlockSpec(memory_space=pl.ANY)] * len(operands),
            out_specs=[pl.BlockSpec(memory_space=pl.ANY)] * outs_n,
            scratch_shapes=piece(2 * slab) + mids() + mids() + piece(2 * slab)
            + [dma((chunks,)), dma((chunks,))]
            + [dma((chunks,))] * 10,
            compiler_params=pltpu.CompilerParams(collective_id=number, has_side_effects=True, vmem_limit_bytes=58 << 20),
            name=f"route_{base}_{cross}",
        )
        return lambda *args: call(*args)

    return lax.switch(which, [variant(base + n, size) for n, size in enumerate(sizes)], *indices, *operands)


def body(state, keys, values, queries, rates, remaining, first_owner, migration):
    devices = lax.axis_size(("seq", "doc"))
    myself = lax.axis_index(("seq", "doc"))
    doc_first = inverse_of(first_owner)
    source_of = inverse_of(migration)
    weights = state[0]
    width = weights.shape[-1]
    block_rows = keys.shape[2]
    piece_rows = block_rows // devices

    def to_owners(section, doc_for_owner):
        blocks = (keys[section, 0], values[section, 0], queries[section, 0])
        split = tuple((member.reshape(devices, piece_rows, width) for member in blocks))
        dealt = move_rows(split)
        reordered = tuple((jnp.take(member, doc_for_owner, axis=0) for member in dealt))
        collected = move_rows(reordered)
        return tuple((member.reshape(block_rows, width) for member in collected))

    slab = devices // 4
    rounds = keys.shape[0]
    routed = None
    finest = SPLIT_OUT * slab * 16
    if devices % 4 == 0 and slab >= 4 and block_rows % finest == 0 and width % 128 == 0:
        sizes = sorted({slab, slab + slab // 4, slab + slab // 2, 2 * slab})
        which = crossing_class(first_owner, sizes)
        cut = lambda block, count, split: block.reshape(count * split, slab, block_rows // (split * slab), width)
        table = [
            (tensor, section * SPLIT_IN + part, section * 3 + tensor, part, 0)
            for section in range(rounds)
            for tensor in range(3)
            for part in range(SPLIT_IN)
        ]
        operands = [cut(block, rounds, SPLIT_IN) for block in (keys, values, queries)]
        routed = route(0, which, sizes, (), [plan(first_owner, doc_first)], operands, table, 3 * rounds, SPLIT_IN, slab)
        routed = [block.reshape(block_rows, width) for block in routed]

    def run_round(section, weights_in, doc_for_owner):
        doc_here = doc_for_owner[myself]
        if routed is None:
            keys_here, values_here, queries_here = to_owners(section, doc_for_owner)
        else:
            keys_here, values_here, queries_here = routed[3 * section : 3 * section + 3]
        rate_here = lax.dynamic_index_in_dim(rates[section], doc_here, 0, keepdims=False)
        updated = fast_update(weights_in, keys_here, values_here, rate_here)
        return (updated, swiglu_apply(updated, queries_here), doc_here)

    updated, result_one, doc_one = run_round(0, weights, doc_first)
    outgoing = result_one.astype(jnp.bfloat16)
    if routed is None:
        dealt_out = send_back(outgoing.reshape(devices, piece_rows, width))
        returned = send_back(jnp.take(dealt_out, first_owner, axis=0))
        round_one = returned.reshape(1, block_rows, width)
    unused, result_two, doc_two = run_round(1, updated, doc_first)
    is_live = remaining[doc_two] >= 2
    masked = jnp.where(is_live, result_two, jnp.float32(0.0)).astype(jnp.bfloat16)
    if routed is None:
        dealt = move_result(masked.reshape(devices, piece_rows, width))
        regrouped = move_result(jnp.take(dealt, source_of, axis=0))
        round_two = regrouped.reshape(1, block_rows, width)
    else:
        table = [(tensor, part, tensor, part, tensor) for part in range(SPLIT_OUT) for tensor in range(2)]
        plans = [plan(doc_first, first_owner), plan(migration, source_of)]
        operands = [cut(block, 1, SPLIT_OUT) for block in (outgoing, masked)]
        moving = devices // 8
        sent = route(len(sizes), which // 2, sizes[1::2], (moving,), plans, operands, table, 2, SPLIT_OUT, slab)
        round_one, round_two = (block.reshape(1, block_rows, width) for block in sent)
    return (round_one, round_two)


def solution(mesh):
    return jax.shard_map(
        body,
        mesh=mesh,
        in_specs=(
            P(("grp", "seq", "doc"), None, None, None),
            P(None, ("grp", "seq", "doc"), None, None),
            P(None, ("grp", "seq", "doc"), None, None),
            P(None, ("grp", "seq", "doc"), None, None),
            P(None, "grp", None),
            P("grp"),
            P("grp"),
            P("grp"),
        ),
        out_specs=(P(("grp", "seq", "doc"), None, None), P(("grp", "seq", "doc"), None, None)),
        check_vma=False,
    )
```
